256 devices in a mesh: src: 32 (over x, z_hi, core), freq: 8 (over y, z_lo).
Axes of the slice: x: 4, y: 4, z: 8 (z_hi: 4, z_lo: 2; z = z_hi * 2 + z_lo), core: 2. Of those that a mesh axis runs over, the one named last changes fastest.
Arguments:
- wave: bfloat16 [2, 512, 128, 1024], P(None, 'src', 'freq'), may hold values from -6 to 6
- live: int32 [512], replicated, may hold values from 128 to 1024, as said below
- vel_index: int32 [2, 1536], replicated, may hold values from 0 to 7
- taps: float32 [2, 8, 128, 9], P(None, None, 'freq')
Outputs:
- image: float32 [2, 512, 1024], P(None, 'src')
- wave_out: bfloat16 [2, 512, 128, 1024], P(None, 'src', 'freq')
The draws below stay inside these ranges and needn't reach their ends.
Inputs may be any that keep to these rules, and one draw needn't show every extreme that they name: `live`: shot 0 has all 1024 columns and shot 1 has 128.
All inputs are finite; a program needn't handle non-finite values.
Results may differ from the reference program's by a relative error of at most 0.0064.
Values may be sent and summed in bfloat16 or wider, within the bound.
A program may use at most 192 MiB of HBM per device.

```python
import jax
import jax.numpy as jnp
from jax import lax

H = 1024
B = 4
NV = 8
DEPTHS = 2
TAPS = 9
SHOTS = 512
FREQS = 128


def draw_live(key, part):
    values = jax.random.randint(key, (SHOTS,), H // 8, H + 1).astype(jnp.int32)
    values = values.at[0].set(H)
    values = values.at[1].set(H // 8)
    return values


def draw_taps(key, part):
    key_angle = jax.random.fold_in(key, 11)
    key_side = jax.random.fold_in(key, 12)
    angle = jax.random.uniform(key_angle, (NV, FREQS), jnp.float32, -3.14159, 3.14159)
    spread = 0.15
    side = jax.random.uniform(key_side, (2, NV, FREQS, TAPS), jnp.float32, -spread, spread)
    centre = jnp.stack([0.8 * jnp.cos(angle), 0.8 * jnp.sin(angle)])[..., None]
    index = jnp.arange(TAPS)[None, None, None, :]
    return jnp.where(index == B, centre, side).astype(jnp.float32)


def set_ends(drawn, key, low, high):
    place = [jax.random.randint(jax.random.fold_in(key, axis), (), 0, length) for axis, length in enumerate(drawn.shape)]
    main_axis = drawn.shape.index(max(drawn.shape))
    next_to = place[:main_axis] + [(place[main_axis] + 1) % drawn.shape[main_axis]] + place[main_axis + 1:]
    return drawn.at[tuple(place)].set(low).at[tuple(next_to)].set(high)


def block_scale(own_key, shape, shards, smallest, top_value):
    loudness, own = 1.0, jax.random.fold_in(own_key, 6)
    for dim, shards_of in shards:
        steps = jnp.exp(jax.random.uniform(jax.random.fold_in(own, dim), (shards_of,), jnp.float32, smallest / len(shards), top_value / len(shards)))
        loudness = loudness * jnp.repeat(steps, shape[dim] // shards_of).reshape([-1 if axis == dim else 1 for axis in range(len(shape))])
    return loudness


def bell_draw(own_key, extent, scale, bound, cuts=(), kind=jnp.bfloat16):
    entries = scale * jax.random.normal(own_key, extent, jnp.float32)
    if cuts:
        entries = entries * block_scale(own_key, extent, cuts, -0.22, 0.18)
    return jnp.clip(entries, -bound, bound).astype(kind)


def setup_inputs(seed: int = 0) -> dict:
    keys = jax.random.split(jax.random.key(seed), 5)
    wave = bell_draw(keys[0], (2, SHOTS, FREQS, H), 1.0, 6.0, ((1, 32), (2, 8)))
    live = draw_live(jax.random.fold_in(keys[4], 71), 0)
    vel_index = set_ends(jax.random.randint(keys[2], (DEPTHS, SHOTS + H), 0, NV), jax.random.fold_in(keys[2], 1), 0, NV - 1).astype(jnp.int32)
    taps = draw_taps(jax.random.fold_in(keys[4], 71), 0)
    return dict(wave=wave, live=live, vel_index=vel_index, taps=taps)


def receiver_step(field, coef):
    half = (coef.shape[3] - 1) // 2
    width = field.shape[2]
    padded = jnp.pad(field, ((0, 0), (0, 0), (half, half)))
    acc_re = jnp.zeros(field.shape[1:], jnp.float32)
    acc_im = jnp.zeros(field.shape[1:], jnp.float32)
    for k in range(coef.shape[3]):
        piece = padded[:, :, k:k + width]
        acc_re = acc_re + coef[0, :, :, k] * piece[0] - coef[1, :, :, k] * piece[1]
        acc_im = acc_im + coef[0, :, :, k] * piece[1] + coef[1, :, :, k] * piece[0]
    return jnp.stack([acc_re, acc_im])


def shot_step(field, coef):
    half = (coef.shape[2] - 1) // 2
    count = field.shape[1]
    width = field.shape[2]
    padded = jnp.pad(field, ((0, 0), (half, half), (half, half)))
    acc_re = jnp.zeros(field.shape[1:], jnp.float32)
    acc_im = jnp.zeros(field.shape[1:], jnp.float32)
    for j in range(coef.shape[2]):
        piece = padded[:, j:j + count, 2 * half - j:2 * half - j + width]
        c_re = coef[0, :, j][:, None]
        c_im = coef[1, :, j][:, None]
        acc_re = acc_re + c_re * piece[0] - c_im * piece[1]
        acc_im = acc_im + c_re * piece[1] + c_im * piece[0]
    return jnp.stack([acc_re, acc_im])


def reference(wave, live, vel_index, taps):
    offsets = jnp.arange(H, dtype=jnp.int32)
    rows = jnp.arange(SHOTS, dtype=jnp.int32)
    mask = (offsets[None, :] < live[:, None])[None]
    position = rows[:, None] + offsets[None, :]

    def one_freq(item):
        slab, table = item
        field = jnp.where(mask, slab, jnp.zeros_like(slab))
        images = []
        for depth in range(DEPTHS):
            velocity = vel_index[depth]
            coef_r = table[:, velocity[position], :]
            after = receiver_step(field.astype(jnp.float32), coef_r).astype(jnp.bfloat16)
            after = lax.optimization_barrier(after)
            after = jnp.where(mask, after, jnp.zeros_like(after))
            coef_s = table[:, velocity[:SHOTS], :]
            moved = shot_step(after.astype(jnp.float32), coef_s).astype(jnp.bfloat16)
            moved = lax.optimization_barrier(moved)
            field = jnp.where(mask, moved, jnp.zeros_like(moved))
            images.append(field[0].astype(jnp.float32))
        return field, jnp.stack(images)

    fields, parts = lax.map(one_freq, (jnp.moveaxis(wave, 2, 0), jnp.moveaxis(taps, 2, 0)))
    image = jnp.sum(parts, axis=0)
    wave_out = jnp.transpose(fields, (1, 2, 0, 3))
    return image, wave_out
```

```python
import functools

import jax
import jax.numpy as jnp
from jax import lax
from jax.experimental import pallas as pl
from jax.experimental.pallas import tpu as pltpu
from jax.sharding import PartitionSpec as P

MESH = pl.DeviceIdType.MESH
LANES = 128
F32 = jnp.float32
BF16 = jnp.bfloat16


def lane_iota(rows=8):
    return lax.broadcasted_iota(jnp.int32, (rows, LANES), 1)


def shifted(load, block, blocks, delta, lane):
    here = load(block)
    if isinstance(delta, int) and delta == 0:
        return here
    if delta > 0:
        other = load(block + 1) if block + 1 < blocks else jnp.zeros_like(here)
        return pltpu.roll(jnp.where(lane < delta, other, here), LANES - delta, 1)
    other = load(block - 1) if block > 0 else jnp.zeros_like(here)
    return pltpu.roll(jnp.where(lane >= LANES + delta, other, here), -delta, 1)


def keep_mask(lane, block, shot, live):
    h = lane + (LANES * block - shot)
    return (h >= 0) & (h < live)


def load_skewed(wave_ref, x_ref, shot, live, blocks):
    data = wave_ref.shape[-1] // LANES
    lane = lane_iota(16)
    for c in range(2):
        prev = jnp.zeros((16, LANES), F32)
        for b in range(blocks):
            if b < data:
                here = wave_ref[c, shot, :, b * LANES : (b + 1) * LANES].astype(F32)
            else:
                here = jnp.zeros((16, LANES), F32)
            moved = pltpu.roll(jnp.where(lane >= LANES - shot, prev, here), shot, 1)
            keep = keep_mask(lane, b, shot, live)
            x_ref[shot, c, :, b * LANES : (b + 1) * LANES] = jnp.where(keep, moved, 0.0)
            prev = here


def receiver_row(x_ref, coef_ref, depth, r_ref, shot, row, live, blocks):
    lane = lane_iota()
    taps = coef_ref.shape[1]
    half = (taps - 1) // 2
    for b in range(blocks):
        cols = slice(b * LANES, (b + 1) * LANES)
        keep = keep_mask(lane, b, shot, live)
        parts = [[], []]
        for part in range(2):
            rows = slice(part * 8, part * 8 + 8)

            def load(c):
                return lambda i: x_ref[shot, c, rows, i * LANES : (i + 1) * LANES]

            acc_re = acc_im = None
            for k in range(taps):
                x_re = shifted(load(0), b, blocks, k - half, lane)
                x_im = shifted(load(1), b, blocks, k - half, lane)
                c_re = coef_ref[depth, k, 0, rows, cols]
                c_im = coef_ref[depth, k, 1, rows, cols]
                re = c_re * x_re - c_im * x_im
                im = c_re * x_im + c_im * x_re
                acc_re = re if acc_re is None else acc_re + re
                acc_im = im if acc_im is None else acc_im + im
            parts[0].append(jnp.where(keep, acc_re, 0.0))
            parts[1].append(jnp.where(keep, acc_im, 0.0))
        for c in range(2):
            r_ref[row, c, :, cols] = jnp.concatenate(parts[c], axis=0).astype(BF16)


def build_coef(table_ref, vseg_ref, coef_ref, depth, blocks):
    taps = coef_ref.shape[1]
    level = lax.broadcasted_iota(jnp.int32, (24, LANES), 0) % 8
    for b in range(blocks):
        cols = slice(b * LANES, (b + 1) * LANES)
        onehot = (vseg_ref[depth : depth + 1, cols] == level).astype(F32).astype(BF16)
        out = jnp.dot(table_ref[...], onehot, preferred_element_type=F32)
        coef_ref[depth, :, :, :, cols] = out.reshape(taps, 2, 16, LANES)


def build_weights(expand_ref, vshot_ref, w_ref, depth, half):
    width = expand_ref.shape[2]
    for s in range(8):
        block = expand_ref[vshot_ref[depth, half * 8 + s]]
        lead, rest = divmod(32 * s, LANES)
        if rest:
            block = pltpu.roll(block, rest, 1)
        block = block.astype(BF16)
        rows = slice(s * 32, s * 32 + 32)
        w_ref[half, rows, :] = jnp.zeros((32, 512), BF16)
        fit = min(width, 512 - lead * LANES)
        w_ref[half, rows, lead * LANES : lead * LANES + fit] = block[:, :fit]


def place_halo(halo_ref, r_ref, row, delta, blocks):
    lane = lane_iota(16)
    for i in range(4):
        for c in range(2):
            load = lambda j: halo_ref[i, c, :, j * LANES : (j + 1) * LANES].astype(F32)
            for b in range(blocks):
                moved = shifted(load, b, blocks, delta, lane)
                r_ref[row + i, c, :, b * LANES : (b + 1) * LANES] = moved.astype(BF16)


def shot_step(w_ref, r_ref, x_ref, live_ref, half, lo, hi):
    lane = lane_iota(16)
    cols = slice(lo * LANES, hi * LANES)
    rhs = r_ref[half * 8 : half * 8 + 16, :, :, cols].reshape(512, (hi - lo) * LANES)
    y = jnp.dot(w_ref[half], rhs, preferred_element_type=F32)
    for s in range(8):
        shot = half * 8 + s
        for b in range(lo, hi):
            keep = keep_mask(lane, b, shot, live_ref[shot])
            for c in range(2):
                part = y[s * 32 + c * 16 : s * 32 + c * 16 + 16, (b - lo) * LANES : (b - lo + 1) * LANES]
                part = part.astype(BF16).astype(F32)
                x_ref[shot, c, :, b * LANES : (b + 1) * LANES] = jnp.where(keep, part, 0.0)


def unskew(load, block, blocks, shot, lane):
    here = load(block)
    if isinstance(shot, int) and shot == 0:
        return here
    other = load(block + 1)
    return pltpu.roll(jnp.where(lane < shot, other, here), LANES - shot, 1)


def put_image(x_ref, image_ref, data):
    for shot in range(x_ref.shape[0]):
        sums = [jnp.sum(x_ref[shot, 0, :, b * LANES : (b + 1) * LANES], axis=0, keepdims=True) for b in range(data + 1)]
        for b in range(data):
            moved = unskew(lambda i: jnp.broadcast_to(sums[i], (8, LANES)), b, data + 1, shot, lane_iota())
            image_ref[shot : shot + 1, b * LANES : (b + 1) * LANES] = moved[:1]


def first_kernel(live_ref, wave_ref, vseg_ref, table_ref, r_ref, x_ref, coef_ref):
    blocks = r_ref.shape[-1] // LANES
    build_coef(table_ref, vseg_ref, coef_ref, 0, blocks)

    def body(shot, carry):
        load_skewed(wave_ref, x_ref, shot, live_ref[shot], blocks)
        receiver_row(x_ref, coef_ref, 0, r_ref, shot, shot, live_ref[shot], blocks)
        return carry

    lax.fori_loop(0, 16, body, 0)


def middle_kernel(live_ref, vshot_ref, vseg_ref, table_ref, expand_ref, r_in_ref, before_ref, after_ref,
                  r_ref, image_ref, x_ref, coef_ref, w_ref, wide_ref):
    blocks = r_ref.shape[-1] // LANES
    data = image_ref.shape[-1] // LANES
    build_coef(table_ref, vseg_ref, coef_ref, 0, blocks)
    for half in range(2):
        build_weights(expand_ref, vshot_ref, w_ref, 0, half)
    wide_ref[4:20] = r_in_ref[...]
    place_halo(before_ref, wide_ref, 0, 16, blocks)
    place_halo(after_ref, wide_ref, 20, -16, blocks)
    for half in range(2):
        for lo in range(0, blocks, 3):
            shot_step(w_ref, wide_ref, x_ref, live_ref, half, lo, lo + 3)

    put_image(x_ref, image_ref, data)

    def body(shot, carry):
        receiver_row(x_ref, coef_ref, 0, r_ref, shot, shot, live_ref[shot], blocks)
        return carry

    lax.fori_loop(0, 16, body, 0)


def last_kernel(live_ref, vshot_ref, expand_ref, r_in_ref, before_ref, after_ref,
                out_ref, image_ref, x_ref, w_ref, wide_ref):
    blocks = wide_ref.shape[-1] // LANES
    data = image_ref.shape[-1] // LANES
    for half in range(2):
        build_weights(expand_ref, vshot_ref, w_ref, 0, half)
    wide_ref[4:20] = r_in_ref[...]
    place_halo(before_ref, wide_ref, 0, 16, blocks)
    place_halo(after_ref, wide_ref, 20, -16, blocks)
    for half in range(2):
        for lo in range(0, blocks, 3):
            shot_step(w_ref, wide_ref, x_ref, live_ref, half, lo, lo + 3)

    put_image(x_ref, image_ref, data)
    lane = lane_iota(16)

    def body(shot, carry):
        for c in range(2):
            load = lambda i: x_ref[shot, c, :, i * LANES : (i + 1) * LANES]
            for b in range(data):
                out_ref[c, shot, :, b * LANES : (b + 1) * LANES] = unskew(load, b, blocks, shot, lane).astype(BF16)
        return carry

    lax.fori_loop(0, 16, body, 0)


def reduce_kernel(peers, first_ref, second_ref, out_ref, parts, got, total, full, sems):
    me = lax.axis_index("freq")
    rows = first_ref.shape[0]
    barrier = pltpu.get_barrier_semaphore()
    for step in range(1, peers):
        pl.semaphore_signal(barrier, inc=1, device_id={"freq": lax.rem(me + step, peers)}, device_id_type=MESH)
    for q in range(peers):
        parts[q, 0:rows, :] = first_ref[:, q * LANES : (q + 1) * LANES]
        parts[q, rows : 2 * rows, :] = second_ref[:, q * LANES : (q + 1) * LANES]
    pl.semaphore_wait(barrier, peers - 1)

    def scatter(step):
        peer = lax.rem(me + step, peers)
        return pltpu.make_async_remote_copy(
            src_ref=parts.at[peer], dst_ref=got.at[step], send_sem=sems.at[0, step], recv_sem=sems.at[1, step],
            device_id={"freq": peer}, device_id_type=MESH)

    def gather(step):
        peer = lax.rem(me + step, peers)
        return pltpu.make_async_remote_copy(
            src_ref=total, dst_ref=full.at[step], send_sem=sems.at[2, step], recv_sem=sems.at[3, step],
            device_id={"freq": peer}, device_id_type=MESH)

    for step in range(1, peers):
        scatter(step).start()
    value = parts[me]
    for step in range(1, peers):
        scatter(step).wait()
        value = value + got[step]
    total[...] = value
    for step in range(1, peers):
        gather(step).start()
    cols = pl.ds(pl.multiple_of(me * LANES, LANES), LANES)
    out_ref[0, :, cols] = value[:rows]
    out_ref[1, :, cols] = value[rows:]
    for step in range(1, peers):
        gather(step).wait()
        owner = lax.rem(me + peers - step, peers)
        cols = pl.ds(pl.multiple_of(owner * LANES, LANES), LANES)
        out_ref[0, :, cols] = full[step, 0:rows, :]
        out_ref[1, :, cols] = full[step, rows : 2 * rows, :]


def split3(value):
    high = lax.reduce_precision(value, 8, 7)
    rest = value - high
    mid = lax.reduce_precision(rest, 8, 7)
    low = rest - mid
    return jnp.concatenate([high, mid, low], axis=-1).astype(BF16)


def tap_tables(taps):
    _, levels, freqs, count = taps.shape
    table = split3(jnp.transpose(taps, (3, 0, 2, 1)).reshape(count * 2 * freqs, levels))
    re, im = taps[0], taps[1]
    mix = jnp.stack([jnp.stack([re, -im], -1), jnp.stack([im, re], -1)], 1)
    same = jnp.eye(freqs, dtype=F32)
    expand = mix[..., None] * same[None, None, :, None, None, :]
    expand = expand.reshape(levels, 2 * freqs, count * 2 * freqs)
    return table, jnp.pad(expand, ((0, 0), (0, 0), (0, 384 - expand.shape[2])))


def local(wave, live, vel_index, taps):
    shots, freqs, width = wave.shape[1:]
    wide = width + LANES
    n_src = lax.axis_size("src")
    n_freq = lax.axis_size("freq")
    first = lax.axis_index("src") * shots
    live_here = lax.dynamic_slice_in_dim(live, first, shots)
    vshot = lax.dynamic_slice_in_dim(vel_index, first, shots, axis=1)
    vseg = lax.dynamic_slice_in_dim(jnp.pad(vel_index, ((0, 0), (0, LANES))), first, wide, axis=1)
    table, expand = tap_tables(taps)

    smem = pl.BlockSpec(memory_space=pltpu.SMEM)
    vmem = pl.BlockSpec(memory_space=pltpu.VMEM)
    x_buf = pltpu.VMEM((shots, 2, freqs, wide), F32)
    coef_buf = pltpu.VMEM((1, taps.shape[3], 2, freqs, wide), F32)
    w_buf = pltpu.VMEM((2, 256, 512), BF16)
    wide_buf = pltpu.VMEM((shots + 8, 2, freqs, wide), BF16)
    r_shape = jax.ShapeDtypeStruct((shots, 2, freqs, wide), BF16)
    image_shape = jax.ShapeDtypeStruct((shots, width), F32)
    up = [(i, i + 1) for i in range(n_src - 1)]
    down = [(i + 1, i) for i in range(n_src - 1)]

    r = pl.pallas_call(
        first_kernel, out_shape=r_shape, in_specs=[smem, vmem, vmem, vmem], out_specs=vmem,
        scratch_shapes=[x_buf, coef_buf],
    )(live_here, wave, vseg[0:1], table)
    before = lax.ppermute(r[shots - 4 :], "src", up)
    after = lax.ppermute(r[:4], "src", down)
    r, image0 = pl.pallas_call(
        middle_kernel, out_shape=(r_shape, image_shape),
        in_specs=[smem, smem] + [vmem] * 6, out_specs=(vmem, vmem),
        scratch_shapes=[x_buf, coef_buf, w_buf, wide_buf],
    )(live_here, vshot[0:1], vseg[1:2], table, expand, r, before, after)
    before = lax.ppermute(r[shots - 4 :], "src", up)
    after = lax.ppermute(r[:4], "src", down)
    wave_out, image1 = pl.pallas_call(
        last_kernel, out_shape=(jax.ShapeDtypeStruct(wave.shape, BF16), image_shape),
        in_specs=[smem, smem] + [vmem] * 4, out_specs=(vmem, vmem),
        scratch_shapes=[x_buf, w_buf, wide_buf],
    )(live_here, vshot[1:2], expand, r, before, after)
    piece = pltpu.VMEM((n_freq, 2 * shots, LANES), F32)
    image = pl.pallas_call(
        functools.partial(reduce_kernel, n_freq),
        out_shape=jax.ShapeDtypeStruct((2, shots, width), F32),
        in_specs=[vmem, vmem], out_specs=vmem,
        scratch_shapes=[piece, piece, pltpu.VMEM((2 * shots, LANES), F32), piece, pltpu.SemaphoreType.DMA((4, n_freq))],
        compiler_params=pltpu.CompilerParams(collective_id=0, has_side_effects=True),
    )(image0, image1)
    return image, wave_out


def solution(mesh):
    placed = (P(None, "src", "freq", None), P(), P(), P(None, None, "freq", None))
    return jax.shard_map(
        local, mesh=mesh, in_specs=placed,
        out_specs=(P(None, "src", None), P(None, "src", "freq", None)), check_vma=False,
    )
```

```python
import functools

import jax
import jax.numpy as jnp
from jax import lax
from jax.experimental import pallas as pl
from jax.experimental.pallas import tpu as pltpu
from jax.sharding import PartitionSpec as P

MESH = pl.DeviceIdType.MESH
LANES = 128
F32 = jnp.float32
BF16 = jnp.bfloat16


def lane_iota(rows=8):
    return lax.broadcasted_iota(jnp.int32, (rows, LANES), 1)


def shifted(load, block, blocks, delta, lane):
    here = load(block)
    if isinstance(delta, int) and delta == 0:
        return here
    if delta > 0:
        other = load(block + 1) if block + 1 < blocks else jnp.zeros_like(here)
        return pltpu.roll(jnp.where(lane < delta, other, here), LANES - delta, 1)
    other = load(block - 1) if block > 0 else jnp.zeros_like(here)
    return pltpu.roll(jnp.where(lane >= LANES + delta, other, here), -delta, 1)


def keep_mask(lane, block, shot, live):
    h = lane + (LANES * block - shot)
    return (h >= 0) & (h < live)


def load_skewed(wave_ref, x_ref, shot, live, blocks):
    data = wave_ref.shape[-1] // LANES
    lane = lane_iota(16)
    for c in range(2):
        prev = jnp.zeros((16, LANES), F32)
        for b in range(blocks):
            if b < data:
                here = wave_ref[c, shot, :, b * LANES : (b + 1) * LANES].astype(F32)
            else:
                here = jnp.zeros((16, LANES), F32)
            moved = pltpu.roll(jnp.where(lane >= LANES - shot, prev, here), shot, 1)
            keep = keep_mask(lane, b, shot, live)
            x_ref[shot, c, :, b * LANES : (b + 1) * LANES] = jnp.where(keep, moved, 0.0)
            prev = here


def receiver_row(x_ref, coef_ref, depth, r_ref, shot, row, live, blocks):
    lane = lane_iota()
    taps = coef_ref.shape[1]
    half = (taps - 1) // 2
    for b in range(blocks):
        cols = slice(b * LANES, (b + 1) * LANES)
        keep = keep_mask(lane, b, shot, live)
        parts = [[], []]
        for part in range(2):
            rows = slice(part * 8, part * 8 + 8)

            def load(c):
                return lambda i: x_ref[shot, c, rows, i * LANES : (i + 1) * LANES]

            acc_re = acc_im = None
            for k in range(taps):
                x_re = shifted(load(0), b, blocks, k - half, lane)
                x_im = shifted(load(1), b, blocks, k - half, lane)
                c_re = coef_ref[depth, k, 0, rows, cols]
                c_im = coef_ref[depth, k, 1, rows, cols]
                re = c_re * x_re - c_im * x_im
                im = c_re * x_im + c_im * x_re
                acc_re = re if acc_re is None else acc_re + re
                acc_im = im if acc_im is None else acc_im + im
            parts[0].append(jnp.where(keep, acc_re, 0.0))
            parts[1].append(jnp.where(keep, acc_im, 0.0))
        for c in range(2):
            r_ref[depth, row, c, :, cols] = jnp.concatenate(parts[c], axis=0).astype(BF16)


def build_tables(taps_ref, row_ref, swap_ref, table_ref, expand_ref):
    _, count, levels, freqs = taps_ref.shape
    row_ref[...] = jnp.zeros_like(row_ref)
    swap_ref[...] = jnp.zeros_like(swap_ref)
    for k in range(count):
        for c in range(2):
            piece = taps_ref[c, k]
            at = (2 * k + c) * freqs
            row_ref[:, at : at + freqs] = piece
            at = (2 * k + 1 - c) * freqs
            swap_ref[:, at : at + freqs] = piece
    row = row_ref[...]
    swap = swap_ref[...]
    high = row.astype(BF16)
    rest = row - high.astype(F32)
    mid = rest.astype(BF16)
    low = (rest - mid.astype(F32)).astype(BF16)
    table_ref[...] = jnp.concatenate([high.astype(F32), mid.astype(F32), low.astype(F32)], axis=0).astype(BF16)
    lane = lax.broadcasted_iota(jnp.int32, row.shape, 1)
    real = jnp.where((lane // freqs) % 2 == 1, -row, row)
    lane = lax.broadcasted_iota(jnp.int32, (freqs, row.shape[1]), 1)
    same = lane % freqs == lax.broadcasted_iota(jnp.int32, (freqs, row.shape[1]), 0)
    for v in range(levels):
        for c, source in enumerate((real, swap)):
            line = jnp.broadcast_to(source[v : v + 1], same.shape)
            expand_ref[v, c * freqs : (c + 1) * freqs, :] = jnp.where(same, line, 0.0)


def build_coef(table_ref, vel_ref, coef_ref, depth, first, blocks):
    taps = coef_ref.shape[1]
    level = lax.broadcasted_iota(jnp.int32, (24, LANES), 0) % 8
    lane = lane_iota(1)
    base = first // LANES
    rest = lax.rem(first, LANES)

    def load(b):
        return vel_ref[depth : depth + 1, pl.ds(pl.multiple_of((base + b) * LANES, LANES), LANES)]

    for b in range(blocks):
        cols = slice(b * LANES, (b + 1) * LANES)
        here = load(b)
        other = load(b + 1) if b + 1 < blocks else here
        line = jnp.broadcast_to(jnp.where(lane < rest, other, here), (8, LANES))
        line = pltpu.roll(line, lax.rem(LANES - rest, LANES), 1)
        onehot = (jnp.concatenate([line] * 3, axis=0) == level).astype(F32).astype(BF16)
        out = lax.dot_general(table_ref[...], onehot, (((0,), (0,)), ((), ())), preferred_element_type=F32)
        coef_ref[depth, :, :, :, cols] = out[: taps * 32].reshape(taps, 2, 16, LANES)


def window_of(shot):
    return 0 if shot < 4 else (4 if shot < 12 else 8)


def build_weights(expand_ref, vel_ref, w_ref, depth, first):
    width = expand_ref.shape[2]
    for shot in range(16):
        block = expand_ref[vel_ref[depth, first + shot]]
        lead, rest = divmod(32 * (shot - window_of(shot)), LANES)
        if rest:
            block = pltpu.roll(block, rest, 1)
        block = block.astype(BF16)
        rows = slice(shot * 32, shot * 32 + 32)
        w_ref[depth, rows, :] = jnp.zeros((32, 512), BF16)
        fit = min(width, 512 - lead * LANES)
        w_ref[depth, rows, lead * LANES : lead * LANES + fit] = block[:, :fit]


def place_halo(halo_ref, r_ref, depth, row, delta, blocks, valid):
    lane = lane_iota(16)

    def body(i, carry):
        for c in range(2):
            load = lambda j: halo_ref[depth, i, c, :, j * LANES : (j + 1) * LANES].astype(F32)
            for b in range(blocks):
                moved = jnp.where(valid, shifted(load, b, blocks, delta, lane), 0.0)
                r_ref[depth, row + i, c, :, b * LANES : (b + 1) * LANES] = moved.astype(BF16)
        return carry

    lax.fori_loop(0, 4, body, 0)


def shot_step(w_ref, r_ref, x_ref, live_ref, first, depth, start, stop, blocks):
    lane = lane_iota(16)
    window = window_of(start)
    for lo in range(0, blocks, 3):
        cols = slice(lo * LANES, (lo + 3) * LANES)
        rhs = r_ref[depth, window : window + 16, :, :, cols].reshape(512, 3 * LANES)
        y = jnp.dot(w_ref[depth, start * 32 : stop * 32, :], rhs, preferred_element_type=F32)
        for shot in range(start, stop):
            at = (shot - start) * 32
            for b in range(3):
                keep = keep_mask(lane, lo + b, shot, live_ref[first + shot])
                for c in range(2):
                    part = y[at + c * 16 : at + c * 16 + 16, b * LANES : (b + 1) * LANES].astype(BF16).astype(F32)
                    x_ref[shot, c, :, (lo + b) * LANES : (lo + b + 1) * LANES] = jnp.where(keep, part, 0.0)


def unskew(load, block, shot, lane):
    here = load(block)
    if isinstance(shot, int) and shot == 0:
        return here
    other = load(block + 1)
    return pltpu.roll(jnp.where(lane < shot, other, here), LANES - shot, 1)


def put_image(x_ref, parts_ref, depth, shots, data):
    for shot in shots:
        sums = [jnp.sum(x_ref[shot, 0, :, b * LANES : (b + 1) * LANES], axis=0, keepdims=True) for b in range(data + 1)]
        for b in range(data):
            moved = unskew(lambda i: jnp.broadcast_to(sums[i], (8, LANES)), b, shot, lane_iota())
            parts_ref[depth, b, shot : shot + 1, :] = moved[:1]


def put_out(x_ref, out_ref, shot, data):
    lane = lane_iota(16)
    for c in range(2):
        load = lambda i: x_ref[shot, c, :, i * LANES : (i + 1) * LANES]
        for b in range(data):
            out_ref[c, shot, :, b * LANES : (b + 1) * LANES] = unskew(load, b, shot, lane).astype(BF16)


def kernel(n_src, n_freq, live_ref, vel_smem, vel_ref, taps_ref, wave_ref, image_ref, out_ref,
           x_ref, coef_ref, wide_ref, before_ref, after_ref, w_ref, row_ref, swap_ref, table_ref, expand_ref,
           parts, got, total, full, halo_sems, image_sems):
    src = lax.axis_index("src")
    me = lax.axis_index("freq")
    shots, freqs = wave_ref.shape[1:3]
    data = wave_ref.shape[-1] // LANES
    blocks = wide_ref.shape[-1] // LANES
    depths = wide_ref.shape[0]
    first = src * shots
    ahead, behind = lax.rem(src + 1, n_src), lax.rem(src + n_src - 1, n_src)

    barrier = pltpu.get_barrier_semaphore()
    for peer in (ahead, behind):
        pl.semaphore_signal(barrier, inc=1, device_id={"src": peer}, device_id_type=MESH)
    for step in range(1, n_freq):
        pl.semaphore_signal(barrier, inc=1, device_id={"freq": lax.rem(me + step, n_freq)}, device_id_type=MESH)

    def halo(depth, side):
        return pltpu.make_async_remote_copy(
            src_ref=wide_ref.at[depth, pl.ds(shots if side == 0 else 4, 4)],
            dst_ref=(before_ref if side == 0 else after_ref).at[depth],
            send_sem=halo_sems.at[0, depth, side], recv_sem=halo_sems.at[1, depth, side],
            device_id={"src": ahead if side == 0 else behind}, device_id_type=MESH)

    def scatter(depth, step):
        peer = lax.rem(me + step, n_freq)
        return pltpu.make_async_remote_copy(
            src_ref=parts.at[depth, peer], dst_ref=got.at[depth, step],
            send_sem=image_sems.at[0, depth, step], recv_sem=image_sems.at[1, depth, step],
            device_id={"freq": peer}, device_id_type=MESH)

    def gather(depth, step):
        peer = lax.rem(me + step, n_freq)
        return pltpu.make_async_remote_copy(
            src_ref=total.at[depth], dst_ref=full.at[depth, step],
            send_sem=image_sems.at[2, depth, step], recv_sem=image_sems.at[3, depth, step],
            device_id={"freq": peer}, device_id_type=MESH)

    def send_parts(depth):
        for step in range(1, n_freq):
            scatter(depth, step).start()

    def send_total(depth):
        value = parts[depth, me]
        for step in range(1, n_freq):
            scatter(depth, step).wait()
            value = value + got[depth, step]
        total[depth] = value
        for step in range(1, n_freq):
            gather(depth, step).start()
        image_ref[depth, :, pl.ds(pl.multiple_of(me * LANES, LANES), LANES)] = value

    def take_total(depth):
        for step in range(1, n_freq):
            gather(depth, step).wait()
            owner = lax.rem(me + n_freq - step, n_freq)
            image_ref[depth, :, pl.ds(pl.multiple_of(owner * LANES, LANES), LANES)] = full[depth, step]

    def first_rows(start, stop, jump):
        def body(i, carry):
            shot = i + jump * (i // 4)
            live = live_ref[first + shot]
            load_skewed(wave_ref, x_ref, shot, live, blocks)
            receiver_row(x_ref, coef_ref, 0, wide_ref, shot, shot + 4, live, blocks)
            return carry

        lax.fori_loop(start, stop, body, 0)

    def next_rows(depth, start, stop, jump):
        def body(i, carry):
            shot = i + jump * (i // 4)
            receiver_row(x_ref, coef_ref, depth, wide_ref, shot, shot + 4, live_ref[first + shot], blocks)
            return carry

        lax.fori_loop(start, stop, body, 0)

    def take_halo(depth):
        halo(depth, 0).wait_recv()
        place_halo(before_ref, wide_ref, depth, 0, 16, blocks, src > 0)
        halo(depth, 1).wait_recv()
        place_halo(after_ref, wide_ref, depth, 20, -16, blocks, src < n_src - 1)

    edges = [0, 1, 2, 3, 12, 13, 14, 15]
    inner = list(range(4, 12))
    build_tables(taps_ref, row_ref, swap_ref, table_ref, expand_ref)
    build_coef(table_ref, vel_ref, coef_ref, 0, first, blocks)
    first_rows(0, 8, 8)
    pl.semaphore_wait(barrier, n_freq + 1)
    halo(0, 0).start()
    halo(0, 1).start()
    first_rows(4, 12, 0)
    build_coef(table_ref, vel_ref, coef_ref, 1, first, blocks)
    for depth in range(depths):
        build_weights(expand_ref, vel_smem, w_ref, depth, first)
    shot_step(w_ref, wide_ref, x_ref, live_ref, first, 0, 4, 12, blocks)
    next_rows(1, 4, 12, 0)
    put_image(x_ref, parts, 0, inner, data)
    take_halo(0)
    shot_step(w_ref, wide_ref, x_ref, live_ref, first, 0, 0, 4, blocks)
    shot_step(w_ref, wide_ref, x_ref, live_ref, first, 0, 12, 16, blocks)
    next_rows(1, 0, 8, 8)
    halo(1, 0).start()
    halo(1, 1).start()
    put_image(x_ref, parts, 0, edges, data)
    send_parts(0)

    def out_rows(start, stop, jump):
        def body(i, carry):
            put_out(x_ref, out_ref, i + jump * (i // 4), data)
            return carry

        lax.fori_loop(start, stop, body, 0)

    shot_step(w_ref, wide_ref, x_ref, live_ref, first, 1, 4, 12, blocks)
    put_image(x_ref, parts, 1, inner, data)
    out_rows(4, 12, 0)
    send_total(0)
    take_halo(1)
    shot_step(w_ref, wide_ref, x_ref, live_ref, first, 1, 0, 4, blocks)
    shot_step(w_ref, wide_ref, x_ref, live_ref, first, 1, 12, 16, blocks)
    put_image(x_ref, parts, 1, edges, data)
    send_parts(1)
    out_rows(0, 8, 8)
    take_total(0)
    send_total(1)
    for depth in range(depths):
        for side in range(2):
            halo(depth, side).wait_send()
    take_total(1)


def local(wave, live, vel_index, taps):
    shots, freqs, width = wave.shape[1:]
    levels, count = taps.shape[1], taps.shape[3]
    depths = vel_index.shape[0]
    wide = width + LANES
    n_src = lax.axis_size("src")
    n_freq = lax.axis_size("freq")
    smem = pl.BlockSpec(memory_space=pltpu.SMEM)
    vmem = pl.BlockSpec(memory_space=pltpu.VMEM)
    halo_buf = pltpu.VMEM((depths, 4, 2, freqs, wide), BF16)
    piece = pltpu.VMEM((depths, n_freq, shots, LANES), F32)
    tap_row = pltpu.VMEM((levels, 384), F32)
    return pl.pallas_call(
        functools.partial(kernel, n_src, n_freq),
        out_shape=(jax.ShapeDtypeStruct((depths, shots, width), F32), jax.ShapeDtypeStruct(wave.shape, BF16)),
        in_specs=[smem, smem, vmem, vmem, vmem], out_specs=(vmem, vmem),
        scratch_shapes=[
            pltpu.VMEM((shots, 2, freqs, wide), F32),
            pltpu.VMEM((depths, count, 2, freqs, wide), F32),
            pltpu.VMEM((depths, shots + 8, 2, freqs, wide), BF16),
            halo_buf, halo_buf,
            pltpu.VMEM((depths, 512, 512), BF16),
            tap_row, tap_row,
            pltpu.VMEM((3 * levels, 384), BF16),
            pltpu.VMEM((levels, 2 * freqs, 384), F32),
            piece, piece, pltpu.VMEM((depths, shots, LANES), F32), piece,
            pltpu.SemaphoreType.DMA((2, depths, 2)),
            pltpu.SemaphoreType.DMA((4, depths, n_freq)),
        ],
        compiler_params=pltpu.CompilerParams(collective_id=0, has_side_effects=True, vmem_limit_bytes=60 * 1024 * 1024),
    )(live, vel_index, vel_index, jnp.transpose(taps, (0, 3, 1, 2)), wave)


def solution(mesh):
    placed = (P(None, "src", "freq", None), P(), P(), P(None, None, "freq", None))
    return jax.shard_map(
        local, mesh=mesh, in_specs=placed,
        out_specs=(P(None, "src", None), P(None, "src", "freq", None)), check_vma=False,
    )
```

```python
import functools

import jax
import jax.numpy as jnp
from jax import lax
from jax.experimental import pallas as pl
from jax.experimental.pallas import tpu as pltpu
from jax.sharding import PartitionSpec as P

MESH = pl.DeviceIdType.MESH
LANES = 128
F32 = jnp.float32
BF16 = jnp.bfloat16


def lane_iota(rows=8):
    return lax.broadcasted_iota(jnp.int32, (rows, LANES), 1)


def shifted(load, block, blocks, delta, lane):
    here = load(block)
    if isinstance(delta, int) and delta == 0:
        return here
    if delta > 0:
        other = load(block + 1) if block + 1 < blocks else jnp.zeros_like(here)
        return pltpu.roll(jnp.where(lane < delta, other, here), LANES - delta, 1)
    other = load(block - 1) if block > 0 else jnp.zeros_like(here)
    return pltpu.roll(jnp.where(lane >= LANES + delta, other, here), -delta, 1)


def keep_mask(lane, block, shot, live):
    h = lane + (LANES * block - shot)
    return (h >= 0) & (h < live)


def load_skewed(wave_ref, x_ref, shot, live, blocks):
    data = wave_ref.shape[-1] // LANES
    lane = lane_iota(16)
    for c in range(2):
        prev = jnp.zeros((16, LANES), F32)
        for b in range(blocks):
            if b < data:
                here = wave_ref[c, shot, :, b * LANES : (b + 1) * LANES].astype(F32)
            else:
                here = jnp.zeros((16, LANES), F32)
            moved = pltpu.roll(jnp.where(lane >= LANES - shot, prev, here), shot, 1)
            keep = keep_mask(lane, b, shot, live)
            x_ref[shot, c, :, b * LANES : (b + 1) * LANES] = jnp.where(keep, moved, 0.0)
            prev = here


def receiver_row(x_ref, coef_ref, depth, r_ref, shot, row, live, blocks):
    lane = lane_iota()
    taps = coef_ref.shape[1]
    half = (taps - 1) // 2
    for b in range(blocks):
        cols = slice(b * LANES, (b + 1) * LANES)
        keep = keep_mask(lane, b, shot, live)
        parts = [[], []]
        for part in range(2):
            rows = slice(part * 8, part * 8 + 8)

            def load(c):
                return lambda i: x_ref[shot, c, rows, i * LANES : (i + 1) * LANES]

            acc_re = acc_im = None
            for k in range(taps):
                x_re = shifted(load(0), b, blocks, k - half, lane)
                x_im = shifted(load(1), b, blocks, k - half, lane)
                c_re = coef_ref[depth, k, 0, rows, cols]
                c_im = coef_ref[depth, k, 1, rows, cols]
                re = c_re * x_re - c_im * x_im
                im = c_re * x_im + c_im * x_re
                acc_re = re if acc_re is None else acc_re + re
                acc_im = im if acc_im is None else acc_im + im
            parts[0].append(jnp.where(keep, acc_re, 0.0))
            parts[1].append(jnp.where(keep, acc_im, 0.0))
        for c in range(2):
            r_ref[depth, row, c, :, cols] = jnp.concatenate(parts[c], axis=0).astype(BF16)


def build_tables(taps_ref, row_ref, swap_ref, table_ref, expand_ref):
    _, count, levels, freqs = taps_ref.shape
    row_ref[...] = jnp.zeros_like(row_ref)
    swap_ref[...] = jnp.zeros_like(swap_ref)
    for k in range(count):
        for c in range(2):
            piece = taps_ref[c, k]
            at = (2 * k + c) * freqs
            row_ref[:, at : at + freqs] = piece
            at = (2 * k + 1 - c) * freqs
            swap_ref[:, at : at + freqs] = piece
    row = row_ref[...]
    swap = swap_ref[...]
    high = row.astype(BF16)
    rest = row - high.astype(F32)
    mid = rest.astype(BF16)
    low = (rest - mid.astype(F32)).astype(BF16)
    table_ref[...] = jnp.concatenate([high.astype(F32), mid.astype(F32), low.astype(F32)], axis=0).astype(BF16)
    lane = lax.broadcasted_iota(jnp.int32, row.shape, 1)
    real = jnp.where((lane // freqs) % 2 == 1, -row, row)
    lane = lax.broadcasted_iota(jnp.int32, (freqs, row.shape[1]), 1)
    same = lane % freqs == lax.broadcasted_iota(jnp.int32, (freqs, row.shape[1]), 0)
    for v in range(levels):
        for c, source in enumerate((real, swap)):
            line = jnp.broadcast_to(source[v : v + 1], same.shape)
            expand_ref[v, c * freqs : (c + 1) * freqs, :] = jnp.where(same, line, 0.0)


def build_coef(table_ref, vel_ref, coef_ref, depth, first, blocks):
    taps = coef_ref.shape[1]
    level = lax.broadcasted_iota(jnp.int32, (24, LANES), 0) % 8
    lane = lane_iota(1)
    base = first // LANES
    rest = lax.rem(first, LANES)

    def load(b):
        return vel_ref[depth : depth + 1, pl.ds(pl.multiple_of((base + b) * LANES, LANES), LANES)]

    for b in range(blocks):
        cols = slice(b * LANES, (b + 1) * LANES)
        here = load(b)
        other = load(b + 1) if b + 1 < blocks else here
        line = jnp.broadcast_to(jnp.where(lane < rest, other, here), (8, LANES))
        line = pltpu.roll(line, lax.rem(LANES - rest, LANES), 1)
        onehot = (jnp.concatenate([line] * 3, axis=0) == level).astype(F32).astype(BF16)
        out = lax.dot_general(table_ref[...], onehot, (((0,), (0,)), ((), ())), preferred_element_type=F32)
        coef_ref[depth, :, :, :, cols] = out[: taps * 32].reshape(taps, 2, 16, LANES)


def window_of(shot):
    return 0 if shot < 4 else (4 if shot < 12 else 8)


def build_weights(expand_ref, vel_ref, w_ref, depth, first):
    width = expand_ref.shape[2]
    for shot in range(16):
        block = expand_ref[vel_ref[depth, first + shot]]
        lead, rest = divmod(32 * (shot - window_of(shot)), LANES)
        if rest:
            block = pltpu.roll(block, rest, 1)
        block = block.astype(BF16)
        rows = slice(shot * 32, shot * 32 + 32)
        w_ref[depth, rows, :] = jnp.zeros((32, 512), BF16)
        fit = min(width, 512 - lead * LANES)
        w_ref[depth, rows, lead * LANES : lead * LANES + fit] = block[:, :fit]


def place_halo(halo_ref, r_ref, depth, i, row, delta, blocks, valid):
    lane = lane_iota(16)
    for c in range(2):
        load = lambda j: halo_ref[depth, i, c, :, j * LANES : (j + 1) * LANES].astype(F32)
        for b in range(blocks):
            moved = jnp.where(valid, shifted(load, b, blocks, delta, lane), 0.0)
            r_ref[depth, row, c, :, b * LANES : (b + 1) * LANES] = moved.astype(BF16)


def shot_step(w_ref, r_ref, x_ref, live_ref, first, depth, start, stop, blocks):
    lane = lane_iota(16)
    window = window_of(start)
    for lo in range(0, blocks, 3):
        cols = slice(lo * LANES, (lo + 3) * LANES)
        rhs = r_ref[depth, window : window + 16, :, :, cols].reshape(512, 3 * LANES)
        y = jnp.dot(w_ref[depth, start * 32 : stop * 32, :], rhs, preferred_element_type=F32)
        for shot in range(start, stop):
            at = (shot - start) * 32
            for b in range(3):
                keep = keep_mask(lane, lo + b, shot, live_ref[first + shot])
                for c in range(2):
                    part = y[at + c * 16 : at + c * 16 + 16, b * LANES : (b + 1) * LANES].astype(BF16).astype(F32)
                    x_ref[shot, c, :, (lo + b) * LANES : (lo + b + 1) * LANES] = jnp.where(keep, part, 0.0)


def unskew(load, block, shot, lane):
    here = load(block)
    if isinstance(shot, int) and shot == 0:
        return here
    other = load(block + 1)
    return pltpu.roll(jnp.where(lane < shot, other, here), LANES - shot, 1)


def put_image(x_ref, parts_ref, depth, shots, data):
    for shot in shots:
        sums = [jnp.sum(x_ref[shot, 0, :, b * LANES : (b + 1) * LANES], axis=0, keepdims=True) for b in range(data + 1)]
        for b in range(data):
            moved = unskew(lambda i: jnp.broadcast_to(sums[i], (8, LANES)), b, shot, lane_iota())
            parts_ref[depth, b, shot : shot + 1, :] = moved[:1]


def put_out(x_ref, out_ref, shot, data):
    lane = lane_iota(16)
    for c in range(2):
        load = lambda i: x_ref[shot, c, :, i * LANES : (i + 1) * LANES]
        for b in range(data):
            out_ref[c, shot, :, b * LANES : (b + 1) * LANES] = unskew(load, b, shot, lane).astype(BF16)


def kernel(n_src, n_freq, live_ref, vel_smem, vel_ref, taps_ref, wave_hbm, image_ref, out_hbm, wave_ref, out_ref,
           x_ref, coef_ref, wide_ref, before_ref, after_ref, w_ref, row_ref, swap_ref, table_ref, expand_ref,
           parts, got, total, full, halo_sems, image_sems, copy_sems):
    src = lax.axis_index("src")
    me = lax.axis_index("freq")
    shots, freqs = wave_ref.shape[1:3]
    data = wave_ref.shape[-1] // LANES
    blocks = wide_ref.shape[-1] // LANES
    depths = wide_ref.shape[0]
    first = src * shots
    ahead, behind = lax.rem(src + 1, n_src), lax.rem(src + n_src - 1, n_src)

    barrier = pltpu.get_barrier_semaphore()
    for peer in (ahead, behind):
        pl.semaphore_signal(barrier, inc=1, device_id={"src": peer}, device_id_type=MESH)
    for step in range(1, n_freq):
        pl.semaphore_signal(barrier, inc=1, device_id={"freq": lax.rem(me + step, n_freq)}, device_id_type=MESH)

    def wave_in(side):
        return pltpu.make_async_copy(wave_hbm.at[side], wave_ref.at[side], copy_sems.at[0, side])

    def wave_back(shot):
        return pltpu.make_async_copy(out_ref.at[:, shot], out_hbm.at[:, shot], copy_sems.at[1, shot])

    for side in range(2):
        wave_in(side).start()

    def halo(depth, side, h):
        return pltpu.make_async_remote_copy(
            src_ref=wide_ref.at[depth, shots + 3 - h if side == 0 else 4 + h],
            dst_ref=before_ref.at[depth, 3 - h] if side == 0 else after_ref.at[depth, h],
            send_sem=halo_sems.at[0, depth, side, h], recv_sem=halo_sems.at[1, depth, side, h],
            device_id={"src": ahead if side == 0 else behind}, device_id_type=MESH)

    def scatter(depth, step):
        peer = lax.rem(me + step, n_freq)
        return pltpu.make_async_remote_copy(
            src_ref=parts.at[depth, peer], dst_ref=got.at[depth, step],
            send_sem=image_sems.at[0, depth, step], recv_sem=image_sems.at[1, depth, step],
            device_id={"freq": peer}, device_id_type=MESH)

    def gather(depth, step):
        peer = lax.rem(me + step, n_freq)
        return pltpu.make_async_remote_copy(
            src_ref=total.at[depth], dst_ref=full.at[depth, step],
            send_sem=image_sems.at[2, depth, step], recv_sem=image_sems.at[3, depth, step],
            device_id={"freq": peer}, device_id_type=MESH)

    def send_parts(depth):
        for step in range(1, n_freq):
            scatter(depth, step).start()

    def send_total(depth):
        value = parts[depth, me]
        for step in range(1, n_freq):
            scatter(depth, step).wait()
            value = value + got[depth, step]
        total[depth] = value
        for step in range(1, n_freq):
            gather(depth, step).start()
        image_ref[depth, :, pl.ds(pl.multiple_of(me * LANES, LANES), LANES)] = value

    def take_total(depth):
        for step in range(1, n_freq):
            gather(depth, step).wait()
            owner = lax.rem(me + n_freq - step, n_freq)
            image_ref[depth, :, pl.ds(pl.multiple_of(owner * LANES, LANES), LANES)] = full[depth, step]

    def first_row(shot):
        live = live_ref[first + shot]
        load_skewed(wave_ref, x_ref, shot, live, blocks)
        receiver_row(x_ref, coef_ref, 0, wide_ref, shot, shot + 4, live, blocks)

    def next_row(shot):
        receiver_row(x_ref, coef_ref, 1, wide_ref, shot, shot + 4, live_ref[first + shot], blocks)

    def inner_rows(step):
        def body(shot, carry):
            step(shot)
            return carry

        lax.fori_loop(4, 12, body, 0)

    def edge_rows(step, depth, start):
        def body(h, carry):
            step(h)
            halo(depth, 1, h).start()
            step(15 - h)
            halo(depth, 0, h).start()
            return carry

        lax.fori_loop(start, 4, body, 0)

    def take_halo(depth):
        def body(h, carry):
            halo(depth, 1, h).wait_recv()
            place_halo(after_ref, wide_ref, depth, h, 20 + h, -16, blocks, src < n_src - 1)
            halo(depth, 0, h).wait_recv()
            place_halo(before_ref, wide_ref, depth, 3 - h, 3 - h, 16, blocks, src > 0)
            return carry

        lax.fori_loop(0, 4, body, 0)

    edges = [0, 1, 2, 3, 12, 13, 14, 15]
    inner = list(range(4, 12))
    build_tables(taps_ref, row_ref, swap_ref, table_ref, expand_ref)
    build_coef(table_ref, vel_ref, coef_ref, 0, first, blocks)
    for side in range(2):
        wave_in(side).wait()
    pl.semaphore_wait(barrier, n_freq + 1)
    edge_rows(first_row, 0, 0)
    inner_rows(first_row)
    build_coef(table_ref, vel_ref, coef_ref, 1, first, blocks)
    for depth in range(depths):
        build_weights(expand_ref, vel_smem, w_ref, depth, first)
    shot_step(w_ref, wide_ref, x_ref, live_ref, first, 0, 4, 12, blocks)
    inner_rows(next_row)
    put_image(x_ref, parts, 0, inner, data)
    take_halo(0)
    shot_step(w_ref, wide_ref, x_ref, live_ref, first, 0, 0, 4, blocks)
    shot_step(w_ref, wide_ref, x_ref, live_ref, first, 0, 12, 16, blocks)
    edge_rows(next_row, 1, 0)
    put_image(x_ref, parts, 0, edges, data)
    send_parts(0)

    def out_rows(start, stop, jump):
        def body(i, carry):
            shot = i + jump * (i // 4)
            put_out(x_ref, out_ref, shot, data)
            wave_back(shot).start()
            return carry

        lax.fori_loop(start, stop, body, 0)

    shot_step(w_ref, wide_ref, x_ref, live_ref, first, 1, 4, 12, blocks)
    put_image(x_ref, parts, 1, inner, data)
    out_rows(4, 12, 0)
    send_total(0)
    take_halo(1)
    shot_step(w_ref, wide_ref, x_ref, live_ref, first, 1, 0, 4, blocks)
    shot_step(w_ref, wide_ref, x_ref, live_ref, first, 1, 12, 16, blocks)
    put_image(x_ref, parts, 1, edges, data)
    send_parts(1)
    out_rows(0, 8, 8)
    take_total(0)
    send_total(1)
    for depth in range(depths):
        for side in range(2):
            for h in range(4):
                halo(depth, side, h).wait_send()
    for shot in range(shots):
        wave_back(shot).wait()
    take_total(1)


def local(wave, live, vel_index, taps):
    shots, freqs, width = wave.shape[1:]
    levels, count = taps.shape[1], taps.shape[3]
    depths = vel_index.shape[0]
    wide = width + LANES
    n_src = lax.axis_size("src")
    n_freq = lax.axis_size("freq")
    smem = pl.BlockSpec(memory_space=pltpu.SMEM)
    vmem = pl.BlockSpec(memory_space=pltpu.VMEM)
    away = pl.BlockSpec(memory_space=pl.ANY)
    halo_buf = pltpu.VMEM((depths, 4, 2, freqs, wide), BF16)
    piece = pltpu.VMEM((depths, n_freq, shots, LANES), F32)
    tap_row = pltpu.VMEM((levels, 384), F32)
    return pl.pallas_call(
        functools.partial(kernel, n_src, n_freq),
        out_shape=(jax.ShapeDtypeStruct((depths, shots, width), F32), jax.ShapeDtypeStruct(wave.shape, BF16)),
        in_specs=[smem, smem, vmem, vmem, away], out_specs=(vmem, away),
        scratch_shapes=[
            pltpu.VMEM(wave.shape, BF16),
            pltpu.VMEM(wave.shape, BF16),
            pltpu.VMEM((shots, 2, freqs, wide), F32),
            pltpu.VMEM((depths, count, 2, freqs, wide), F32),
            pltpu.VMEM((depths, shots + 8, 2, freqs, wide), BF16),
            halo_buf, halo_buf,
            pltpu.VMEM((depths, 512, 512), BF16),
            tap_row, tap_row,
            pltpu.VMEM((3 * levels, 384), BF16),
            pltpu.VMEM((levels, 2 * freqs, 384), F32),
            piece, piece, pltpu.VMEM((depths, shots, LANES), F32), piece,
            pltpu.SemaphoreType.DMA((2, depths, 2, 4)),
            pltpu.SemaphoreType.DMA((4, depths, n_freq)),
            pltpu.SemaphoreType.DMA((2, shots)),
        ],
        compiler_params=pltpu.CompilerParams(collective_id=0, has_side_effects=True, vmem_limit_bytes=60 * 1024 * 1024),
    )(live, vel_index, vel_index, jnp.transpose(taps, (0, 3, 1, 2)), wave)


def solution(mesh):
    placed = (P(None, "src", "freq", None), P(), P(), P(None, None, "freq", None))
    return jax.shard_map(
        local, mesh=mesh, in_specs=placed,
        out_specs=(P(None, "src", None), P(None, "src", "freq", None)), check_vma=False,
    )
```
